512 devices in a mesh: inp: 128 (over y, z, core), vis: 4 (over x).
Axes of the slice: x: 4, y: 8, z: 8, core: 2. Of those that a mesh axis runs over, the one named last changes fastest.
Arguments:
- samples: bfloat16 [128, 2048, 2048], P('vis', 'inp'), may hold values from -6 to 6
- history: bfloat16 [3, 2048, 2048], P(None, 'inp'), may hold values from -6 to 6
- fir_taps: float32 [4, 2048], replicated, may hold values from -3 to 3
- kept_channels: int32 [128], replicated, may hold values from 0 to 1023, as said below
Outputs:
- visibility: bfloat16 [128, 2048, 2048], P('inp', 'vis')
The draws below stay inside these ranges and needn't reach their ends.
Inputs may be any that keep to these rules, and one draw needn't show every extreme that they name: `kept_channels`: 128 distinct channel numbers in no particular order; channels 0 and 1023 are always among them.
All inputs are finite; a program needn't handle non-finite values.
Results may differ from the reference program's by a relative error of at most 0.0078.
Values may be sent and summed in bfloat16 or wider, within the bound.
A program may use at most 64 MiB of HBM per device.

```python
import math
import jax
import jax.numpy as jnp
from jax import lax

INPUTS = 2048
CHANNELS = 1024
TAPS = 4
SAMPLES = 2048
KEEP = 128
FRAMES = 128


def draw_kept_channels(key, part):
    inner = jax.random.permutation(key, CHANNELS - 2)[:KEEP - 2].astype(jnp.int32) + 1
    chosen = jnp.concatenate([jnp.array([0, CHANNELS - 1], jnp.int32), inner])
    return jax.random.permutation(jax.random.fold_in(key, 7), chosen).astype(jnp.int32)


def block_scale(own_key, extent, pieces, least, high):
    def one(axis_at, blocks):
        heights = jax.random.uniform(jax.random.fold_in(jax.random.fold_in(own_key, 6), axis_at), (blocks,), jnp.float32, least / len(pieces), high / len(pieces))
        return jnp.repeat(jnp.exp(heights), extent[axis_at] // blocks).reshape((-1,) + (1,) * (len(extent) - axis_at - 1))

    gain = one(*pieces[0])
    for cut in pieces[1:]:
        gain = gain * one(*cut)
    return gain


def centred(key, shape, spread, most, cuts=(), held_as=jnp.bfloat16):
    drawn = spread * jax.random.normal(key, shape, jnp.float32)
    if cuts:
        drawn = drawn * block_scale(key, shape, cuts, -0.22, 0.18)
    return jnp.clip(drawn, -most, most).astype(held_as)


def setup_inputs(seed: int = 0) -> dict:
    splits = jax.random.split(jax.random.key(seed), 5)
    samples = centred(splits[0], (FRAMES, INPUTS, SAMPLES), 1.0, 6.0, ((0, 4), (1, 128)))
    history = centred(splits[1], (TAPS - 1, INPUTS, SAMPLES), 1.0, 6.0, ((1, 128),))
    fir_taps = centred(splits[2], (TAPS, SAMPLES), 0.5, 3.0, (), jnp.float32)
    kept_channels = draw_kept_channels(jax.random.fold_in(splits[4], 71), 0)
    return dict(samples=samples, history=history, fir_taps=fir_taps, kept_channels=kept_channels)


def make_table(kept_channels, sample_count):
    positions = jnp.arange(sample_count, dtype=jnp.int32)
    products = kept_channels.astype(jnp.int32)[:, None] * positions[None, :] % sample_count
    angles = products.astype(jnp.float32) * (2.0 * math.pi / sample_count)
    norm_scale = 1.0 / math.sqrt(sample_count)
    table = jnp.concatenate([jnp.cos(angles) * norm_scale, -jnp.sin(angles) * norm_scale], axis=0)
    return table.astype(jnp.bfloat16)

def reference(samples, history, fir_taps, kept_channels):
    dft_table = make_table(kept_channels, SAMPLES)

    def one_frame(frame):
        weighted = jnp.zeros((INPUTS, SAMPLES), jnp.float32)
        for tap_index in range(TAPS):
            source = frame - (TAPS - 1) + tap_index
            from_window = lax.dynamic_index_in_dim(samples, jnp.maximum(source, 0).astype(jnp.int32), 0, keepdims=False)
            from_history = lax.dynamic_index_in_dim(history, jnp.clip(source + TAPS - 1, 0, TAPS - 2).astype(jnp.int32), 0, keepdims=False)
            chosen = jnp.where(source >= 0, from_window, from_history)
            weighted = weighted + fir_taps[tap_index][None, :] * chosen.astype(jnp.float32)
        weighted = weighted.astype(jnp.bfloat16)
        return jnp.dot(dft_table, weighted.T, preferred_element_type=jnp.float32).astype(jnp.bfloat16)
    spectra = lax.map(one_frame, jnp.arange(FRAMES, dtype=jnp.int32))

    def one_channel(channel):
        real_part = lax.dynamic_index_in_dim(spectra, channel, 1, keepdims=False)
        imag_part = lax.dynamic_index_in_dim(spectra, channel + KEEP, 1, keepdims=False)
        re_sum = jnp.dot(real_part.T, real_part, preferred_element_type=jnp.float32) + jnp.dot(imag_part.T, imag_part, preferred_element_type=jnp.float32)
        im_sum = jnp.dot(imag_part.T, real_part, preferred_element_type=jnp.float32) - jnp.dot(real_part.T, imag_part, preferred_element_type=jnp.float32)
        row_ids = jnp.arange(INPUTS, dtype=jnp.int32)
        upper = row_ids[None, :] >= row_ids[:, None]
        return (jnp.where(upper, re_sum, im_sum) / float(FRAMES)).astype(jnp.bfloat16)
    return lax.map(one_channel, jnp.arange(KEEP, dtype=jnp.int32))
```

```python
import functools
import math

import jax
import jax.numpy as jnp
from jax import lax
from jax.experimental import pallas as pl
from jax.experimental.pallas import tpu as pltpu
from jax.sharding import PartitionSpec as P

TAPS = 4
MESH = pl.DeviceIdType.MESH
NI, NV, NY, NZ = 128, 4, 8, 8
ZGROUPS = ((0,), (1, 7), (2, 6), (3, 5), (4,))
DEPTH = 1


def exchange_kernel(z_ref, g_ref, a_send, a_recv, l_sem, x_send, x_recv):
    me = lax.axis_index("inp")
    v = lax.axis_index("vis")
    y, z, c = me // 16, lax.rem(me // 2, 8), lax.rem(me, 2)
    right, left, opp = lax.rem(v + 1, NV), lax.rem(v + 3, NV), lax.rem(v + 2, NV)

    barrier = pltpu.get_barrier_semaphore()

    def greet(d, _):
        pl.semaphore_signal(barrier, inc=1, device_id=(lax.rem(me + d, NI), v), device_id_type=MESH)
        return 0

    lax.fori_loop(1, NI, greet, 0)
    for other in (left, right):
        pl.semaphore_signal(barrier, inc=1, device_id=(me, other), device_id_type=MESH)
    pl.semaphore_wait(barrier, NI - 1 + 2)

    own = pltpu.make_async_copy(z_ref.at[me], g_ref.at[v, y, z, c], l_sem)
    own.start()

    def send(dy, dz, dc):
        ty, tz, tc = lax.rem(y + dy, 8), lax.rem(z + dz, 8), lax.rem(c + dc, 2)
        pltpu.make_async_remote_copy(
            src_ref=z_ref.at[ty * 16 + tz * 2 + tc],
            dst_ref=g_ref.at[v, y, z, c],
            send_sem=a_send,
            recv_sem=a_recv.at[(8 - dz) % 8],
            device_id=(ty * 16 + tz * 2 + tc, v),
            device_id_type=MESH,
        ).start()

    for group in ZGROUPS:
        if group == (0,):
            send(0, 0, 1)

        def body(dy, _, group=group):
            for dc in (0, 1):
                for dz in group:
                    send(dy, dz, dc)
            return 0

        lax.fori_loop(1 if group == (0,) else 0, 8, body, 0)
    own.wait()

    def whole(vv, tz):
        return g_ref.at[vv, :, tz]

    def half(vv, tz, h):
        return g_ref.at[vv, pl.ds(4 * h, 4), tz]

    def relay(k):
        for dz in ZGROUPS[k]:
            tz = lax.rem(z + dz, 8)
            for side, (source, target) in enumerate(((left, right), (right, left))):
                pltpu.make_async_copy(whole(source, tz), whole(source, tz), x_recv.at[dz, side]).wait()
                pltpu.make_async_remote_copy(
                    src_ref=half(source, tz, side),
                    dst_ref=half(source, tz, side),
                    send_sem=x_send.at[2],
                    recv_sem=x_recv.at[dz, 2 + side],
                    device_id=(me, target),
                    device_id_type=MESH,
                ).start()

    for k, group in enumerate(ZGROUPS):
        for dz in group:
            tz = lax.rem(z + dz, 8)
            if dz == 0:
                pltpu.make_async_copy(z_ref.at[pl.ds(0, 15)], z_ref.at[pl.ds(0, 15)], a_recv.at[0]).wait()
            else:
                pltpu.make_async_copy(whole(v, tz), whole(v, tz), a_recv.at[dz]).wait()
            for side, target in enumerate((right, left)):
                pltpu.make_async_remote_copy(
                    src_ref=whole(v, tz),
                    dst_ref=whole(v, tz),
                    send_sem=x_send.at[side],
                    recv_sem=x_recv.at[dz, side],
                    device_id=(me, target),
                    device_id_type=MESH,
                ).start()
        if k >= DEPTH:
            relay(k - DEPTH)
    for k in range(len(ZGROUPS) - DEPTH, len(ZGROUPS)):
        relay(k)
    for dz in range(8):
        tz = lax.rem(z + dz, 8)
        for side in range(2):
            pltpu.make_async_copy(half(opp, tz, side), half(opp, tz, side), x_recv.at[dz, 2 + side]).wait()
    for i in range(3):
        pltpu.make_async_copy(g_ref.at[v], g_ref.at[v], x_send.at[i]).wait()
    pltpu.make_async_copy(z_ref.at[pl.ds(0, NI - 1)], z_ref.at[pl.ds(0, NI - 1)], a_send).wait()


def exchange(blocks):
    return pl.pallas_call(
        exchange_kernel,
        out_shape=jax.ShapeDtypeStruct((NV, NY, NZ, 2, 8, 128), jnp.bfloat16),
        in_specs=[pl.BlockSpec(memory_space=pltpu.VMEM)],
        out_specs=pl.BlockSpec(memory_space=pltpu.VMEM),
        scratch_shapes=[
            pltpu.SemaphoreType.DMA,
            pltpu.SemaphoreType.DMA((8,)),
            pltpu.SemaphoreType.DMA,
            pltpu.SemaphoreType.DMA((3,)),
            pltpu.SemaphoreType.DMA((8, 4)),
        ],
        compiler_params=pltpu.CompilerParams(collective_id=0, has_side_effects=True),
    )(blocks)


def make_table(kept_channels, sample_count):
    low = jnp.arange(128, dtype=jnp.int32)
    high = jnp.arange(sample_count // 128, dtype=jnp.int32) * 128
    step = 2.0 * math.pi / sample_count

    def pair(n):
        angle = (kept_channels[:, None] * n[None, :] % sample_count).astype(jnp.float32) * step
        return jnp.cos(angle), jnp.sin(angle)

    (cl, sl), (ch, sh) = pair(low), pair(high)
    scale = 1.0 / math.sqrt(sample_count)
    cl, sl = (cl * scale)[:, None, :], (sl * scale)[:, None, :]
    ch, sh = ch[:, :, None], sh[:, :, None]
    real = ch * cl - sh * sl
    imag = -(sh * cl + ch * sl)
    count = kept_channels.shape[0]
    return jnp.concatenate([real, imag], axis=0).reshape(2 * count, sample_count).astype(jnp.bfloat16)


def shifted(value, axis, steps):
    count = lax.axis_size(axis)
    initial, last = (max(0, -steps), min(count, count - steps))
    return lax.ppermute(value, axis, [(source, source + steps) for source in range(initial, last)])


def per_device(samples, history, fir_taps, kept_channels):
    vis_index = lax.axis_index("vis")
    frame_count, input_count, sample_count = samples.shape
    previous = shifted(samples[frame_count - TAPS + 1 :], "vis", 1)
    previous = jnp.where(vis_index == 0, history, previous)
    extended = jnp.concatenate([previous, samples], axis=0)
    weighted = fir_taps[0][None, None, :] * extended[0:frame_count].astype(jnp.float32)
    for tap_index in range(1, TAPS):
        weighted = weighted + fir_taps[tap_index][None, None, :] * extended[
            tap_index : tap_index + frame_count
        ].astype(jnp.float32)
    weighted = weighted.astype(jnp.bfloat16)
    table = make_table(kept_channels, sample_count)
    spectra = jnp.einsum("kn,fin->kfi", table, weighted, preferred_element_type=jnp.float32)
    spectra = spectra.astype(jnp.bfloat16).reshape(2, NI, frame_count, 2, 8)
    blocks = spectra.transpose(1, 4, 0, 3, 2).reshape(NI, 8, 128)
    gathered = exchange(blocks)

    gathered = gathered.reshape(NV, NI, 8, 2, 2, frame_count)
    parts = gathered.transpose(3, 1, 4, 2, 0, 5).reshape(2, NI * input_count, NV * frame_count)
    real, imag = parts[0], parts[1]
    rows = NI * input_count // NV
    both = jnp.concatenate([real, imag], axis=1)
    turned = jnp.concatenate([-imag, real], axis=1)
    block = lax.dynamic_slice_in_dim(both, vis_index * rows, rows, 0)
    dims = (((1,), (1,)), ((), ()))
    re_block = lax.dot_general(block, both, dims, preferred_element_type=jnp.float32)
    im_block = lax.dot_general(block, turned, dims, preferred_element_type=jnp.float32)
    row_ids = vis_index * rows + jnp.arange(rows, dtype=jnp.int32)
    col_ids = jnp.arange(NI * input_count, dtype=jnp.int32)
    out = jnp.where(col_ids[None, :] >= row_ids[:, None], re_block, im_block)
    return (out / float(NV * frame_count)).astype(jnp.bfloat16)[None]


def solution(mesh):
    return jax.shard_map(
        per_device,
        mesh=mesh,
        in_specs=(P("vis", "inp", None), P(None, "inp", None), P(), P()),
        out_specs=P("inp", "vis", None),
        check_vma=False,
    )
```

```python
import functools
import math

import jax
import jax.numpy as jnp
from jax import lax
from jax.experimental import pallas as pl
from jax.experimental.pallas import tpu as pltpu
from jax.sharding import PartitionSpec as P

TAPS = 4
SAMPLES, FRAMES, ROWS = 2048, 32, 512
MESH = pl.DeviceIdType.MESH
NI, NV, NY, NZ = 128, 4, 8, 8
ZGROUPS = ((0,), (1, 7), (2, 6), (3, 5), (4,))
DEPTH = 1


def trig(m):
    quadrant = (m + 256) >> 9
    x = (m - (quadrant << 9)).astype(jnp.float32) * (2.0 * math.pi / SAMPLES)
    s = x * x
    c = 1.0 + s * (-0.5 + s * (1.0 / 24 + s * (-1.0 / 720 + s * (1.0 / 40320))))
    d = x * (1.0 + s * (-1.0 / 6 + s * (1.0 / 120 + s * (-1.0 / 5040 + s * (1.0 / 362880)))))
    odd = (quadrant & 1) == 1
    cos = jnp.where(odd, d, c)
    sin = jnp.where(odd, c, d)
    cos = jnp.where((quadrant == 1) | (quadrant == 2), -cos, cos)
    sin = jnp.where((quadrant == 2) | (quadrant == 3), -sin, sin)
    return cos, sin


def write_table(kept_ref, table_ref):
    lane = lax.broadcasted_iota(jnp.int32, (NI, 128), 1)
    here = lane == lax.broadcasted_iota(jnp.int32, (NI, 128), 0)
    kept = jnp.broadcast_to(kept_ref[...], (NI, 128)).astype(jnp.float32)
    kept = jnp.sum(jnp.where(here, kept, 0.0), axis=1, keepdims=True).astype(jnp.int32)
    cl, sl = trig((kept * lane) & (SAMPLES - 1))
    ch, sh = trig((kept * lane * 128) & (SAMPLES - 1))
    scale = 1.0 / math.sqrt(SAMPLES)
    cl, sl = cl * scale, sl * scale
    for high in range(SAMPLES // 128):
        a = jnp.broadcast_to(ch[:, high : high + 1], (NI, 128))
        b = jnp.broadcast_to(sh[:, high : high + 1], (NI, 128))
        cols = slice(high * 128, high * 128 + 128)
        table_ref[0:NI, cols] = (a * cl - b * sl).astype(jnp.bfloat16)
        table_ref[NI:, cols] = (-(b * cl) - a * sl).astype(jnp.bfloat16)


def write_order(order_ref):
    m = lax.broadcasted_iota(jnp.int32, (512, 512), 0)
    t = lax.broadcasted_iota(jnp.int32, (512, 512), 1)
    source = ((t & 31) << 4) | (((t >> 6) & 1) << 3) | ((t >> 7) << 1) | ((t >> 5) & 1)
    order_ref[...] = jnp.where(m == source, 1.0, 0.0).astype(jnp.bfloat16)


def filter_frames(source_ref, previous_ref, taps_ref, weighted_ref, first, last, lo, hi):
    def chunk(j, _):
        cols = pl.ds(pl.multiple_of(j * 128, 128), 128)
        taps = [jnp.broadcast_to(taps_ref[t : t + 1, cols], (16, 128)) for t in range(TAPS)]
        window = [previous_ref[k, :, cols].astype(jnp.float32) for k in range(TAPS - 1)]
        for f in range(first, last):
            window.append(source_ref[f, :, cols].astype(jnp.float32))
            total = taps[0] * window[0]
            for t in range(1, TAPS):
                total = total + taps[t] * window[t]
            weighted_ref[f * 16 : f * 16 + 16, cols] = total.astype(jnp.bfloat16)
            window = window[1:]
        return 0

    lax.fori_loop(lo, hi, chunk, 0)


def write_blocks(table_ref, weighted_ref, order_ref, wide_ref, z_ref):
    nt = (((1,), (1,)), ((), ()))
    spectra = lax.dot_general(table_ref[...], weighted_ref[...], nt, preferred_element_type=jnp.float32)
    spectra = spectra.astype(jnp.bfloat16)
    spectra = jnp.dot(spectra, order_ref[...], preferred_element_type=jnp.float32)
    even = (lax.broadcasted_iota(jnp.int32, (NI, 128), 1) & 32) == 0
    for pair in range(4):
        cols = slice(pair * 128, pair * 128 + 128)
        re, im = spectra[0:NI, cols], spectra[NI:, cols]
        wide_ref[pl.ds(2 * pair, NI, stride=8), :] = jnp.where(even, re, pltpu.roll(im, 32, 1))
        wide_ref[pl.ds(2 * pair + 1, NI, stride=8), :] = jnp.where(even, pltpu.roll(re, 96, 1), im)
    z_ref[...] = wide_ref[...].reshape(NI, 8, 128).astype(jnp.bfloat16)


def correlate_kernel(g_ref, out_ref, all_ref, re_ref, im_ref):
    j = pl.program_id(0)
    v = lax.axis_index("vis")

    @pl.when(j == 0)
    def _():
        first = lax.broadcasted_iota(jnp.int32, (128, 16, 128), 2) < 64
        low = lax.broadcasted_iota(jnp.int32, (128, 8, 128), 2) < 64
        for pair in range(2):
            a = g_ref[2 * pair].astype(jnp.float32)
            b = g_ref[2 * pair + 1].astype(jnp.float32)
            top = jnp.where(low, a, pltpu.roll(b, 64, 2))
            bottom = jnp.where(low, pltpu.roll(a, 64, 2), b)
            rows = jnp.concatenate([top, bottom], axis=1).reshape(2048, 128)
            all_ref[:, pair * 128 : pair * 128 + 128] = rows.astype(jnp.bfloat16)
        own = all_ref[pl.ds(pl.multiple_of(v * ROWS, ROWS), ROWS), :].astype(jnp.float32)
        re_ref[...] = own.astype(jnp.bfloat16)
        real = (lax.broadcasted_iota(jnp.int32, (ROWS, 128), 1) & 32) == 0
        for pair in range(2):
            x = own[:, pair * 128 : pair * 128 + 128]
            turned = jnp.where(real, pltpu.roll(x, 96, 1), -pltpu.roll(x, 32, 1))
            im_ref[:, pair * 128 : pair * 128 + 128] = turned.astype(jnp.bfloat16)

    nt = (((1,), (1,)), ((), ()))
    cols = all_ref[pl.ds(pl.multiple_of(j * ROWS, ROWS), ROWS), :]
    scale = 1.0 / (NV * FRAMES)

    @pl.when(j > v)
    def _():
        out_ref[0] = (lax.dot_general(re_ref[...], cols, nt, preferred_element_type=jnp.float32) * scale).astype(jnp.bfloat16)

    @pl.when(j < v)
    def _():
        out_ref[0] = (lax.dot_general(im_ref[...], cols, nt, preferred_element_type=jnp.float32) * scale).astype(jnp.bfloat16)

    @pl.when(j == v)
    def _():
        re = lax.dot_general(re_ref[...], cols, nt, preferred_element_type=jnp.float32)
        im = lax.dot_general(im_ref[...], cols, nt, preferred_element_type=jnp.float32)
        row = lax.broadcasted_iota(jnp.int32, (ROWS, ROWS), 0)
        col = lax.broadcasted_iota(jnp.int32, (ROWS, ROWS), 1)
        out_ref[0] = (jnp.where(col >= row, re, im) * scale).astype(jnp.bfloat16)


def correlate(gathered):
    return pl.pallas_call(
        correlate_kernel,
        grid=(NV,),
        out_shape=jax.ShapeDtypeStruct((1, ROWS, NV * ROWS), jnp.bfloat16),
        in_specs=[pl.BlockSpec((NV, NI, 8, 128), lambda j: (0, 0, 0, 0))],
        out_specs=pl.BlockSpec((1, ROWS, ROWS), lambda j: (0, 0, j)),
        scratch_shapes=[
            pltpu.VMEM((NV * ROWS, 256), jnp.bfloat16),
            pltpu.VMEM((ROWS, 256), jnp.bfloat16),
            pltpu.VMEM((ROWS, 256), jnp.bfloat16),
        ],
    )(gathered)


def channelize_kernel(
    samples_ref, history_ref, taps_ref, kept_ref, g_ref,
    frames_ref, previous_ref, table_ref, weighted_ref, order_ref, wide_ref, z_ref,
    load_sem, h_send, h_recv, gossip, a_send, a_recv, x_send, x_recv,
):
    me = lax.axis_index("inp")
    v = lax.axis_index("vis")
    y, z, c = me // 16, lax.rem(me // 2, 8), lax.rem(me, 2)
    right, left, opp = lax.rem(v + 1, NV), lax.rem(v + 3, NV), lax.rem(v + 2, NV)

    def place(dy, dz, dc):
        return lax.rem(y + dy, 8) * 16 + lax.rem(z + dz, 8) * 2 + lax.rem(c + dc, 2)

    barrier = pltpu.get_barrier_semaphore()
    for step in ((1, 0, 0), (7, 0, 0), (0, 1, 0), (0, 7, 0), (0, 0, 1)):
        pl.semaphore_signal(barrier, inc=1, device_id=(place(*step), v), device_id_type=MESH)
    for other in (left, right):
        pl.semaphore_signal(barrier, inc=1, device_id=(me, other), device_id_type=MESH)
    load = pltpu.make_async_copy(samples_ref, frames_ref, load_sem.at[0])
    load.start()
    write_table(kept_ref, table_ref)
    pl.semaphore_wait(barrier, 7)

    tail = samples_ref.at[pl.ds(FRAMES - TAPS + 1, TAPS - 1)]
    handover = pltpu.make_async_remote_copy(
        src_ref=tail, dst_ref=previous_ref, send_sem=h_send, recv_sem=h_recv, device_id=(me, right), device_id_type=MESH
    )
    own_history = pltpu.make_async_copy(history_ref, previous_ref, load_sem.at[1])

    @pl.when(v < NV - 1)
    def _():
        handover.start()

    @pl.when(v == 0)
    def _():
        own_history.start()

    def tell(k, *step):
        pl.semaphore_signal(gossip.at[k], inc=1, device_id=(place(*step), v), device_id_type=MESH)

    def hear(*ks):
        for k in ks:
            pl.semaphore_wait(gossip.at[k], 1)

    def tell_y():
        tell(0, 1, 0, 0)
        tell(1, 7, 0, 0)

    def tell_z():
        tell(2, 0, 1, 0)
        tell(3, 0, 7, 0)

    tell_y()
    write_order(order_ref)
    load.wait()

    def filter_part(lo, hi):
        filter_frames(frames_ref, frames_ref, taps_ref, weighted_ref, TAPS - 1, FRAMES, lo, hi)

    hear(0, 1)
    tell_y()
    filter_part(0, 4)
    hear(0, 1)
    tell_y()
    filter_part(4, 8)
    hear(0, 1)
    tell(4, 0, 0, 1)
    filter_part(8, 12)
    hear(4)
    tell_z()
    filter_part(12, 16)

    @pl.when(v == 0)
    def _():
        own_history.wait()

    @pl.when(v > 0)
    def _():
        handover.wait_recv()

    filter_frames(frames_ref, previous_ref, taps_ref, weighted_ref, 0, TAPS - 1, 0, 16)
    write_blocks(table_ref, weighted_ref, order_ref, wide_ref, z_ref)

    @pl.when(v < NV - 1)
    def _():
        handover.wait_send()

    own = pltpu.make_async_copy(z_ref.at[me], g_ref.at[v, y, z, c], load_sem.at[2])
    own.start()

    def send(dy, dz, dc):
        target = place(dy, dz, dc)
        pltpu.make_async_remote_copy(
            src_ref=z_ref.at[target],
            dst_ref=g_ref.at[v, y, z, c],
            send_sem=a_send,
            recv_sem=a_recv.at[(8 - dz) % 8],
            device_id=(target, v),
            device_id_type=MESH,
        ).start()

    for k, group in enumerate(ZGROUPS):
        if k == 0:
            send(0, 0, 1)
        else:
            hear(2, 3)
            if k < 4:
                tell_z()

        def body(dy, _, group=group):
            for dc in (0, 1):
                for dz in group:
                    send(dy, dz, dc)
            return 0

        lax.fori_loop(1 if k == 0 else 0, 8, body, 0)
    own.wait()

    def whole(vv, tz):
        return g_ref.at[vv, :, tz]

    def half(vv, tz, h):
        return g_ref.at[vv, pl.ds(4 * h, 4), tz]

    def relay(k):
        for dz in ZGROUPS[k]:
            tz = lax.rem(z + dz, 8)
            for side, (source, target) in enumerate(((left, right), (right, left))):
                pltpu.make_async_copy(whole(source, tz), whole(source, tz), x_recv.at[dz, side]).wait()
                pltpu.make_async_remote_copy(
                    src_ref=half(source, tz, side),
                    dst_ref=half(source, tz, side),
                    send_sem=x_send.at[2],
                    recv_sem=x_recv.at[dz, 2 + side],
                    device_id=(me, target),
                    device_id_type=MESH,
                ).start()

    for k, group in enumerate(ZGROUPS):
        for dz in group:
            tz = lax.rem(z + dz, 8)
            if dz == 0:
                pltpu.make_async_copy(z_ref.at[pl.ds(0, 15)], z_ref.at[pl.ds(0, 15)], a_recv.at[0]).wait()
            else:
                pltpu.make_async_copy(whole(v, tz), whole(v, tz), a_recv.at[dz]).wait()
            for side, target in enumerate((right, left)):
                pltpu.make_async_remote_copy(
                    src_ref=whole(v, tz),
                    dst_ref=whole(v, tz),
                    send_sem=x_send.at[side],
                    recv_sem=x_recv.at[dz, side],
                    device_id=(me, target),
                    device_id_type=MESH,
                ).start()
        if k >= DEPTH:
            relay(k - DEPTH)
    for k in range(len(ZGROUPS) - DEPTH, len(ZGROUPS)):
        relay(k)
    for dz in range(8):
        tz = lax.rem(z + dz, 8)
        for side in range(2):
            pltpu.make_async_copy(half(opp, tz, side), half(opp, tz, side), x_recv.at[dz, 2 + side]).wait()
    for i in range(3):
        pltpu.make_async_copy(g_ref.at[v], g_ref.at[v], x_send.at[i]).wait()
    pltpu.make_async_copy(z_ref.at[pl.ds(0, NI - 1)], z_ref.at[pl.ds(0, NI - 1)], a_send).wait()


def channelize(samples, history, fir_taps, kept_channels):
    vmem = pl.BlockSpec(memory_space=pltpu.VMEM)
    hbm = pl.BlockSpec(memory_space=pl.ANY)
    return pl.pallas_call(
        channelize_kernel,
        out_shape=jax.ShapeDtypeStruct((NV, NY, NZ, 2, 8, 128), jnp.bfloat16),
        in_specs=[hbm, hbm, vmem, vmem],
        out_specs=vmem,
        scratch_shapes=[
            pltpu.VMEM((FRAMES, 16, SAMPLES), jnp.bfloat16),
            pltpu.VMEM((TAPS - 1, 16, SAMPLES), jnp.bfloat16),
            pltpu.VMEM((2 * NI, SAMPLES), jnp.bfloat16),
            pltpu.VMEM((512, SAMPLES), jnp.bfloat16),
            pltpu.VMEM((512, 512), jnp.bfloat16),
            pltpu.VMEM((1024, 128), jnp.float32),
            pltpu.VMEM((NI, 8, 128), jnp.bfloat16),
            pltpu.SemaphoreType.DMA((3,)),
            pltpu.SemaphoreType.DMA,
            pltpu.SemaphoreType.DMA,
            pltpu.SemaphoreType.REGULAR((5,)),
            pltpu.SemaphoreType.DMA,
            pltpu.SemaphoreType.DMA((8,)),
            pltpu.SemaphoreType.DMA((3,)),
            pltpu.SemaphoreType.DMA((8, 4)),
        ],
        compiler_params=pltpu.CompilerParams(collective_id=0, has_side_effects=True),
    )(samples, history, fir_taps, kept_channels.reshape(1, NI))


def per_device(samples, history, fir_taps, kept_channels):
    gathered = channelize(samples, history, fir_taps, kept_channels)
    return correlate(gathered.reshape(NV, NI, 8, 128))


def solution(mesh):
    return jax.shard_map(
        per_device,
        mesh=mesh,
        in_specs=(P("vis", "inp", None), P(None, "inp", None), P(), P()),
        out_specs=P("inp", "vis", None),
        check_vma=False,
    )
```

```python
import functools
import math

import jax
import jax.numpy as jnp
from jax import lax
from jax.experimental import pallas as pl
from jax.experimental.pallas import tpu as pltpu
from jax.sharding import PartitionSpec as P

TAPS = 4
SAMPLES, FRAMES, ROWS = 2048, 32, 512
MESH = pl.DeviceIdType.MESH
NI, NV, NY, NZ = 128, 4, 8, 8
ZGROUPS = ((0,), (1, 7), (2, 6), (3, 5), (4,))
DEPTH = 1
DIRECT = (0, 1, 2, 3, 4, 5, 6, 7)


def trig(m):
    quadrant = (m + 256) >> 9
    x = (m - (quadrant << 9)).astype(jnp.float32) * (2.0 * math.pi / SAMPLES)
    s = x * x
    c = 1.0 + s * (-0.5 + s * (1.0 / 24 + s * (-1.0 / 720 + s * (1.0 / 40320))))
    d = x * (1.0 + s * (-1.0 / 6 + s * (1.0 / 120 + s * (-1.0 / 5040 + s * (1.0 / 362880)))))
    odd = (quadrant & 1) == 1
    cos = jnp.where(odd, d, c)
    sin = jnp.where(odd, c, d)
    cos = jnp.where((quadrant == 1) | (quadrant == 2), -cos, cos)
    sin = jnp.where((quadrant == 2) | (quadrant == 3), -sin, sin)
    return cos, sin


def write_table(kept_ref, table_ref):
    lane = lax.broadcasted_iota(jnp.int32, (NI, 128), 1)
    here = lane == lax.broadcasted_iota(jnp.int32, (NI, 128), 0)
    kept = jnp.broadcast_to(kept_ref[...], (NI, 128)).astype(jnp.float32)
    kept = jnp.sum(jnp.where(here, kept, 0.0), axis=1, keepdims=True).astype(jnp.int32)
    cl, sl = trig((kept * lane) & (SAMPLES - 1))
    ch, sh = trig((kept * lane * 128) & (SAMPLES - 1))
    scale = 1.0 / math.sqrt(SAMPLES)
    cl, sl = cl * scale, sl * scale
    for high in range(SAMPLES // 128):
        a = jnp.broadcast_to(ch[:, high : high + 1], (NI, 128))
        b = jnp.broadcast_to(sh[:, high : high + 1], (NI, 128))
        cols = slice(high * 128, high * 128 + 128)
        table_ref[0:NI, cols] = (a * cl - b * sl).astype(jnp.bfloat16)
        table_ref[NI:, cols] = (-(b * cl) - a * sl).astype(jnp.bfloat16)


def write_order(order_ref):
    m = lax.broadcasted_iota(jnp.int32, (512, 512), 0)
    t = lax.broadcasted_iota(jnp.int32, (512, 512), 1)
    source = ((t & 31) << 4) | (((t >> 6) & 1) << 3) | ((t >> 7) << 1) | ((t >> 5) & 1)
    order_ref[...] = jnp.where(m == source, 1.0, 0.0).astype(jnp.bfloat16)


def filter_frames(source_ref, taps_ref, weighted_ref, lo, hi):
    def chunk(j, _):
        cols = pl.ds(pl.multiple_of(j * 128, 128), 128)
        taps = [jnp.broadcast_to(taps_ref[t : t + 1, cols], (16, 128)) for t in range(TAPS)]
        window = []
        for f in range(FRAMES):
            window.append(source_ref[f, :, cols].astype(jnp.float32))
            window = window[-TAPS:]
            terms = taps[TAPS - len(window) :]
            total = terms[0] * window[0]
            for t in range(1, len(window)):
                total = total + terms[t] * window[t]
            weighted_ref[f * 16 : f * 16 + 16, cols] = total.astype(jnp.bfloat16)
        return 0

    lax.fori_loop(lo, hi, chunk, 0)


def write_tail(last, taps_ref, table_ref, spill_ref, tail_ref):
    def chunk(j, _):
        cols = pl.ds(pl.multiple_of(j * 128, 128), 128)
        taps = [jnp.broadcast_to(taps_ref[t : t + 1, cols], (16, 128)) for t in range(TAPS - 1)]
        window = [last(k, cols).astype(jnp.float32) for k in range(TAPS - 1)]
        for f in range(TAPS - 1):
            total = taps[0] * window[f]
            for t in range(1, TAPS - 1 - f):
                total = total + taps[t] * window[f + t]
            spill_ref[f * 16 : f * 16 + 16, cols] = total.astype(jnp.bfloat16)
        return 0

    lax.fori_loop(0, SAMPLES // 128, chunk, 0)
    nt = (((1,), (1,)), ((), ()))
    tail = lax.dot_general(spill_ref[...], table_ref[...], nt, preferred_element_type=jnp.float32)
    tail_ref[...] = tail.astype(jnp.bfloat16)


def write_blocks(table_ref, weighted_ref, head_ref, order_ref, wide_ref, z_ref):
    nt = (((1,), (1,)), ((), ()))
    spectra = lax.dot_general(table_ref[...], weighted_ref[...], nt, preferred_element_type=jnp.float32)
    count = (TAPS - 1) * 16
    place = lax.broadcasted_iota(jnp.int32, (count, 128), 0) == lax.broadcasted_iota(jnp.int32, (count, 128), 1)
    place = jnp.where(place, 1.0, 0.0).astype(jnp.bfloat16)
    tn = (((0,), (0,)), ((), ()))
    first = spectra[:, 0:128] + lax.dot_general(head_ref[...], place, tn, preferred_element_type=jnp.float32)
    spectra = jnp.concatenate([first, spectra[:, 128:]], axis=1).astype(jnp.bfloat16)
    spectra = jnp.dot(spectra, order_ref[...], preferred_element_type=jnp.float32)
    even = (lax.broadcasted_iota(jnp.int32, (NI, 128), 1) & 32) == 0
    for pair in range(4):
        cols = slice(pair * 128, pair * 128 + 128)
        re, im = spectra[0:NI, cols], spectra[NI:, cols]
        wide_ref[pl.ds(2 * pair, NI, stride=8), :] = jnp.where(even, re, pltpu.roll(im, 32, 1))
        wide_ref[pl.ds(2 * pair + 1, NI, stride=8), :] = jnp.where(even, pltpu.roll(re, 96, 1), im)
    z_ref[...] = wide_ref[...].reshape(NI, 8, 128).astype(jnp.bfloat16)


def correlate_kernel(rows_ref, out_ref, im_ref, stage_ref, sem):
    v = lax.axis_index("vis")
    own = rows_ref.at[pl.ds(pl.multiple_of(v * ROWS, ROWS), ROWS)]
    real = (lax.broadcasted_iota(jnp.int32, (ROWS, 128), 1) & 32) == 0
    for pair in range(2):
        x = own[:, pair * 128 : pair * 128 + 128].astype(jnp.float32)
        turned = jnp.where(real, pltpu.roll(x, 96, 1), -pltpu.roll(x, 32, 1))
        im_ref[:, pair * 128 : pair * 128 + 128] = turned.astype(jnp.bfloat16)

    nt = (((1,), (1,)), ((), ()))
    scale = 1.0 / (NV * FRAMES)
    for j in range(NV):
        cols = slice(j * ROWS, j * ROWS + ROWS)

        def product(ref, cols=cols):
            return lax.dot_general(ref[...], rows_ref[cols, :], nt, preferred_element_type=jnp.float32) * scale

        @pl.when(v < j)
        def _():
            stage_ref[j] = product(own).astype(jnp.bfloat16)

        @pl.when(v > j)
        def _():
            stage_ref[j] = product(im_ref).astype(jnp.bfloat16)

        @pl.when(v == j)
        def _():
            row = lax.broadcasted_iota(jnp.int32, (ROWS, ROWS), 0)
            col = lax.broadcasted_iota(jnp.int32, (ROWS, ROWS), 1)
            stage_ref[j] = jnp.where(col >= row, product(own), product(im_ref)).astype(jnp.bfloat16)

        pltpu.make_async_copy(stage_ref.at[j], out_ref.at[0, :, pl.ds(j * ROWS, ROWS)], sem.at[j]).start()
    for j in range(NV):
        pltpu.make_async_copy(stage_ref.at[j], out_ref.at[0, :, pl.ds(j * ROWS, ROWS)], sem.at[j]).wait()


def correlate(rows):
    return pl.pallas_call(
        correlate_kernel,
        out_shape=jax.ShapeDtypeStruct((1, ROWS, NV * ROWS), jnp.bfloat16),
        in_specs=[pl.BlockSpec(memory_space=pltpu.VMEM)],
        out_specs=pl.BlockSpec(memory_space=pl.ANY),
        scratch_shapes=[
            pltpu.VMEM((ROWS, 256), jnp.bfloat16),
            pltpu.VMEM((NV, ROWS, ROWS), jnp.bfloat16),
            pltpu.SemaphoreType.DMA((NV,)),
        ],
    )(rows)


def channelize_kernel(
    samples_ref, history_ref, taps_ref, kept_ref, out_ref,
    frames_ref, previous_ref, table_ref, weighted_ref, order_ref, wide_ref, z_ref, g_ref, stage_ref, spill_ref, tail_ref, head_ref,
    load_sem, h_send, h_recv, gossip, a_send, a_recv, x_send, x_recv, out_sem,
):
    me = lax.axis_index("inp")
    v = lax.axis_index("vis")
    y, z, c = me // 16, lax.rem(me // 2, 8), lax.rem(me, 2)
    right, left, opp = lax.rem(v + 1, NV), lax.rem(v + 3, NV), lax.rem(v + 2, NV)

    def place(dy, dz, dc):
        return lax.rem(y + dy, 8) * 16 + lax.rem(z + dz, 8) * 2 + lax.rem(c + dc, 2)

    barrier = pltpu.get_barrier_semaphore()

    def greet(dy, _):
        for dc in (0, 1):
            pl.semaphore_signal(barrier, inc=1, device_id=(place(dy, 0, dc), v), device_id_type=MESH)
        return 0

    lax.fori_loop(1, NY, greet, 0)
    for step in ((0, 0, 1), (0, 1, 0), (0, 7, 0)):
        pl.semaphore_signal(barrier, inc=1, device_id=(place(*step), v), device_id_type=MESH)
    for other in (left, right, opp):
        pl.semaphore_signal(barrier, inc=1, device_id=(me, other), device_id_type=MESH)

    load = pltpu.make_async_copy(samples_ref, frames_ref, load_sem.at[0])
    load.start()
    old = pltpu.make_async_copy(history_ref, previous_ref, load_sem.at[1])
    old.start()
    write_order(order_ref)
    write_table(kept_ref, table_ref)
    def tell_z():
        pl.semaphore_signal(gossip.at[0], inc=1, device_id=(place(0, 1, 0), v), device_id_type=MESH)
        pl.semaphore_signal(gossip.at[1], inc=1, device_id=(place(0, 7, 0), v), device_id_type=MESH)

    def hear_z():
        pl.semaphore_wait(gossip.at[0], 1)
        pl.semaphore_wait(gossip.at[1], 1)

    load.wait()
    write_tail(lambda k, cols: frames_ref[FRAMES - TAPS + 1 + k, :, cols], taps_ref, table_ref, spill_ref, tail_ref)
    old.wait()

    @pl.when(v == 0)
    def _():
        write_tail(lambda k, cols: previous_ref[k, :, cols], taps_ref, table_ref, spill_ref, head_ref)

    handover = pltpu.make_async_remote_copy(
        src_ref=tail_ref, dst_ref=head_ref, send_sem=h_send, recv_sem=h_recv, device_id=(me, right), device_id_type=MESH
    )

    filter_frames(frames_ref, taps_ref, weighted_ref, 0, 4)
    pl.semaphore_wait(barrier, 2 * (NY - 1) + 6)
    tell_z()

    @pl.when(v < NV - 1)
    def _():
        handover.start()

    filter_frames(frames_ref, taps_ref, weighted_ref, 4, 16)

    @pl.when(v > 0)
    def _():
        handover.wait_recv()

    write_blocks(table_ref, weighted_ref, head_ref, order_ref, wide_ref, z_ref)

    @pl.when(v < NV - 1)
    def _():
        handover.wait_send()
    own = pltpu.make_async_copy(z_ref.at[me], g_ref.at[v, y, z, c], load_sem.at[2])
    own.start()

    def send(target, dz):
        pltpu.make_async_remote_copy(
            src_ref=z_ref.at[target],
            dst_ref=g_ref.at[v, y, z, c],
            send_sem=a_send,
            recv_sem=a_recv.at[(8 - dz) % 8],
            device_id=(target, v),
            device_id_type=MESH,
        ).start()

    for k, group in enumerate(ZGROUPS):
        bases = [(dz, lax.rem(z + dz, NZ) * 2) for dz in group]
        if k == 0:
            send(place(0, 0, 1), 0)
        else:
            hear_z()
            if k < 4:
                tell_z()

        def body(i, _, bases=bases):
            row = lax.rem(y + 8 + (i + 1) // 2 * (2 * lax.rem(i, 2) - 1), NY) * 16
            for core in (0, 1):
                for dz, base in bases:
                    send(row + base + core, dz)
            return 0

        lax.fori_loop(1 if k == 0 else 0, NY, body, 0)
    own.wait()

    def whole(vv, tz):
        return g_ref.at[vv, :, tz]

    def half(vv, tz, h):
        return g_ref.at[vv, pl.ds(4 * h, 4), tz]

    def relay(k):
        for dz in ZGROUPS[k]:
            if dz in DIRECT:
                continue
            tz = lax.rem(z + dz, 8)
            for side, (source, target) in enumerate(((left, right), (right, left))):
                pltpu.make_async_copy(whole(source, tz), whole(source, tz), x_recv.at[dz, side]).wait()
                pltpu.make_async_remote_copy(
                    src_ref=half(source, tz, side),
                    dst_ref=half(source, tz, side),
                    send_sem=x_send.at[2],
                    recv_sem=x_recv.at[dz, 2 + side],
                    device_id=(me, target),
                    device_id_type=MESH,
                ).start()

    for k, group in enumerate(ZGROUPS):
        for dz in group:
            tz = lax.rem(z + dz, 8)
            if dz == 0:
                pltpu.make_async_copy(z_ref.at[pl.ds(0, 15)], z_ref.at[pl.ds(0, 15)], a_recv.at[0]).wait()
            else:
                pltpu.make_async_copy(whole(v, tz), whole(v, tz), a_recv.at[dz]).wait()
            for side, target in enumerate((right, left)):
                pltpu.make_async_remote_copy(
                    src_ref=whole(v, tz),
                    dst_ref=whole(v, tz),
                    send_sem=x_send.at[side],
                    recv_sem=x_recv.at[dz, side],
                    device_id=(me, target),
                    device_id_type=MESH,
                ).start()
            if dz in DIRECT:
                pltpu.make_async_remote_copy(
                    src_ref=whole(v, tz),
                    dst_ref=whole(v, tz),
                    send_sem=x_send.at[2],
                    recv_sem=x_recv.at[dz, 2],
                    device_id=(me, opp),
                    device_id_type=MESH,
                ).start()
        if k >= DEPTH:
            relay(k - DEPTH)
    for k in range(len(ZGROUPS) - DEPTH, len(ZGROUPS)):
        relay(k)
    low = lax.broadcasted_iota(jnp.int32, (2, 8, 128), 2) < 64
    for k, dz in enumerate(dz for group in ZGROUPS for dz in group):
        tz = lax.rem(z + dz, 8)
        if dz in DIRECT:
            for side, source in enumerate((left, right, opp)):
                pltpu.make_async_copy(whole(source, tz), whole(source, tz), x_recv.at[dz, side]).wait()
        else:
            for side in range(2):
                pltpu.make_async_copy(half(opp, tz, side), half(opp, tz, side), x_recv.at[dz, 2 + side]).wait()

        def rows(row, _, k=k, tz=tz):
            for pair in range(2):
                p = g_ref[2 * pair, row, tz].astype(jnp.float32)
                q = g_ref[2 * pair + 1, row, tz].astype(jnp.float32)
                top = jnp.where(low, p, pltpu.roll(q, 64, 2))
                bottom = jnp.where(low, pltpu.roll(p, 64, 2), q)
                both = jnp.concatenate([top, bottom], axis=1).reshape(32, 128)
                stage_ref[k, row, :, pair * 128 : pair * 128 + 128] = both.astype(jnp.bfloat16)
            return 0

        lax.fori_loop(0, NY, rows, 0)
        pltpu.make_async_copy(stage_ref.at[k], out_ref.at[:, tz], out_sem).start()
    pltpu.make_async_copy(stage_ref, out_ref, out_sem).wait()
    for i in range(3):
        pltpu.make_async_copy(g_ref.at[v], g_ref.at[v], x_send.at[i]).wait()
    pltpu.make_async_copy(z_ref.at[pl.ds(0, NI - 1)], z_ref.at[pl.ds(0, NI - 1)], a_send).wait()


def channelize(samples, history, fir_taps, kept_channels):
    vmem = pl.BlockSpec(memory_space=pltpu.VMEM)
    hbm = pl.BlockSpec(memory_space=pl.ANY)
    return pl.pallas_call(
        channelize_kernel,
        out_shape=jax.ShapeDtypeStruct((NY, NZ, 32, 256), jnp.bfloat16),
        in_specs=[hbm, hbm, vmem, vmem],
        out_specs=hbm,
        scratch_shapes=[
            pltpu.VMEM((FRAMES, 16, SAMPLES), jnp.bfloat16),
            pltpu.VMEM((TAPS - 1, 16, SAMPLES), jnp.bfloat16),
            pltpu.VMEM((2 * NI, SAMPLES), jnp.bfloat16),
            pltpu.VMEM((512, SAMPLES), jnp.bfloat16),
            pltpu.VMEM((512, 512), jnp.bfloat16),
            pltpu.VMEM((1024, 128), jnp.float32),
            pltpu.VMEM((NI, 8, 128), jnp.bfloat16),
            pltpu.VMEM((NV, NY, NZ, 2, 8, 128), jnp.bfloat16),
            pltpu.VMEM((NZ, NY, 32, 256), jnp.bfloat16),
            pltpu.VMEM((48, SAMPLES), jnp.bfloat16),
            pltpu.VMEM((48, 2 * NI), jnp.bfloat16),
            pltpu.VMEM((48, 2 * NI), jnp.bfloat16),
            pltpu.SemaphoreType.DMA((3,)),
            pltpu.SemaphoreType.DMA,
            pltpu.SemaphoreType.DMA,
            pltpu.SemaphoreType.REGULAR((2,)),
            pltpu.SemaphoreType.DMA,
            pltpu.SemaphoreType.DMA((8,)),
            pltpu.SemaphoreType.DMA((3,)),
            pltpu.SemaphoreType.DMA((8, 4)),
            pltpu.SemaphoreType.DMA,
        ],
        compiler_params=pltpu.CompilerParams(collective_id=0, has_side_effects=True),
    )(samples, history, fir_taps, kept_channels.reshape(1, NI))


def per_device(samples, history, fir_taps, kept_channels):
    rows = channelize(samples, history, fir_taps, kept_channels)
    return correlate(rows.reshape(NV * ROWS, 256))


def solution(mesh):
    return jax.shard_map(
        per_device,
        mesh=mesh,
        in_specs=(P("vis", "inp", None), P(None, "inp", None), P(), P()),
        out_specs=P("inp", "vis", None),
        check_vma=False,
    )
```

```python
import functools
import math

import jax
import jax.numpy as jnp
from jax import lax
from jax.experimental import pallas as pl
from jax.experimental.pallas import tpu as pltpu
from jax.sharding import PartitionSpec as P

TAPS = 4
SAMPLES, FRAMES, ROWS = 2048, 32, 512
MESH = pl.DeviceIdType.MESH
NI, NV, NY, NZ = 128, 4, 8, 8
ZGROUPS = ((0,), (1, 7), (2, 6), (3, 5), (4,))
DEPTH = 1
DIRECT = (0, 1, 2, 3, 4, 5, 6, 7)


def trig(m):
    quadrant = (m + 256) >> 9
    x = (m - (quadrant << 9)).astype(jnp.float32) * (2.0 * math.pi / SAMPLES)
    s = x * x
    c = 1.0 + s * (-0.5 + s * (1.0 / 24 + s * (-1.0 / 720 + s * (1.0 / 40320))))
    d = x * (1.0 + s * (-1.0 / 6 + s * (1.0 / 120 + s * (-1.0 / 5040 + s * (1.0 / 362880)))))
    odd = (quadrant & 1) == 1
    cos = jnp.where(odd, d, c)
    sin = jnp.where(odd, c, d)
    cos = jnp.where((quadrant == 1) | (quadrant == 2), -cos, cos)
    sin = jnp.where((quadrant == 2) | (quadrant == 3), -sin, sin)
    return cos, sin


def write_table(kept_ref, table_ref):
    lane = lax.broadcasted_iota(jnp.int32, (NI, 128), 1)
    here = lane == lax.broadcasted_iota(jnp.int32, (NI, 128), 0)
    kept = jnp.broadcast_to(kept_ref[...], (NI, 128)).astype(jnp.float32)
    kept = jnp.sum(jnp.where(here, kept, 0.0), axis=1, keepdims=True).astype(jnp.int32)
    cl, sl = trig((kept * lane) & (SAMPLES - 1))
    ch, sh = trig((kept * lane * 128) & (SAMPLES - 1))
    scale = 1.0 / math.sqrt(SAMPLES)
    cl, sl = cl * scale, sl * scale
    for high in range(SAMPLES // 128):
        a = jnp.broadcast_to(ch[:, high : high + 1], (NI, 128))
        b = jnp.broadcast_to(sh[:, high : high + 1], (NI, 128))
        cols = slice(high * 128, high * 128 + 128)
        table_ref[0:NI, cols] = (a * cl - b * sl).astype(jnp.bfloat16)
        table_ref[NI:, cols] = (-(b * cl) - a * sl).astype(jnp.bfloat16)


def write_order(order_ref):
    m = lax.broadcasted_iota(jnp.int32, (512, 512), 0)
    t = lax.broadcasted_iota(jnp.int32, (512, 512), 1)
    source = ((t & 31) << 4) | (((t >> 6) & 1) << 3) | ((t >> 7) << 1) | ((t >> 5) & 1)
    order_ref[...] = jnp.where(m == source, 1.0, 0.0).astype(jnp.bfloat16)


def filter_frames(source_ref, taps_ref, weighted_ref, lo, hi):
    def chunk(j, _):
        cols = pl.ds(pl.multiple_of(j * 128, 128), 128)
        taps = [jnp.broadcast_to(taps_ref[t : t + 1, cols], (16, 128)) for t in range(TAPS)]
        window = []
        for f in range(FRAMES):
            window.append(source_ref[f, :, cols].astype(jnp.float32))
            window = window[-TAPS:]
            terms = taps[TAPS - len(window) :]
            total = terms[0] * window[0]
            for t in range(1, len(window)):
                total = total + terms[t] * window[t]
            weighted_ref[f * 16 : f * 16 + 16, cols] = total.astype(jnp.bfloat16)
        return 0

    lax.fori_loop(lo, hi, chunk, 0)


def write_tail(last, taps_ref, table_ref, spill_ref, tail_ref):
    def chunk(j, _):
        cols = pl.ds(pl.multiple_of(j * 128, 128), 128)
        taps = [jnp.broadcast_to(taps_ref[t : t + 1, cols], (16, 128)) for t in range(TAPS - 1)]
        window = [last(k, cols).astype(jnp.float32) for k in range(TAPS - 1)]
        for f in range(TAPS - 1):
            total = taps[0] * window[f]
            for t in range(1, TAPS - 1 - f):
                total = total + taps[t] * window[f + t]
            spill_ref[f * 16 : f * 16 + 16, cols] = total.astype(jnp.bfloat16)
        return 0

    lax.fori_loop(0, SAMPLES // 128, chunk, 0)
    nt = (((1,), (1,)), ((), ()))
    tail = lax.dot_general(spill_ref[...], table_ref[...], nt, preferred_element_type=jnp.float32)
    tail_ref[...] = tail.astype(jnp.bfloat16)


def write_blocks(table_ref, weighted_ref, head_ref, order_ref, wide_ref, z_ref):
    nt = (((1,), (1,)), ((), ()))
    spectra = lax.dot_general(table_ref[...], weighted_ref[...], nt, preferred_element_type=jnp.float32)
    count = (TAPS - 1) * 16
    place = lax.broadcasted_iota(jnp.int32, (count, 128), 0) == lax.broadcasted_iota(jnp.int32, (count, 128), 1)
    place = jnp.where(place, 1.0, 0.0).astype(jnp.bfloat16)
    tn = (((0,), (0,)), ((), ()))
    first = spectra[:, 0:128] + lax.dot_general(head_ref[...], place, tn, preferred_element_type=jnp.float32)
    spectra = jnp.concatenate([first, spectra[:, 128:]], axis=1).astype(jnp.bfloat16)
    spectra = jnp.dot(spectra, order_ref[...], preferred_element_type=jnp.float32)
    even = (lax.broadcasted_iota(jnp.int32, (NI, 128), 1) & 32) == 0
    for pair in range(4):
        cols = slice(pair * 128, pair * 128 + 128)
        re, im = spectra[0:NI, cols], spectra[NI:, cols]
        wide_ref[pl.ds(2 * pair, NI, stride=8), :] = jnp.where(even, re, pltpu.roll(im, 32, 1))
        wide_ref[pl.ds(2 * pair + 1, NI, stride=8), :] = jnp.where(even, pltpu.roll(re, 96, 1), im)
    z_ref[...] = wide_ref[...].reshape(NI, 8, 128).astype(jnp.bfloat16)


def correlate_kernel(source_ref, out_ref, own, rows_ref, im_ref, stage_ref, sem, load_sem):
    v = lax.axis_index("vis")
    mine = pltpu.make_async_copy(source_ref.at[pl.ds(pl.multiple_of(v * ROWS, ROWS), ROWS)], own, load_sem.at[NV])
    mine.start()
    loads = []
    for j in range(NV):
        block = pl.ds(j * ROWS, ROWS)
        loads.append(pltpu.make_async_copy(source_ref.at[block], rows_ref.at[block], load_sem.at[j]))
        loads[j].start()
    mine.wait()
    real = (lax.broadcasted_iota(jnp.int32, (ROWS, 128), 1) & 32) == 0
    for pair in range(2):
        x = own[:, pair * 128 : pair * 128 + 128].astype(jnp.float32)
        turned = jnp.where(real, pltpu.roll(x, 96, 1), -pltpu.roll(x, 32, 1))
        im_ref[:, pair * 128 : pair * 128 + 128] = turned.astype(jnp.bfloat16)

    nt = (((1,), (1,)), ((), ()))
    scale = 1.0 / (NV * FRAMES)
    for j in range(NV):
        cols = slice(j * ROWS, j * ROWS + ROWS)
        loads[j].wait()

        def product(ref, cols=cols):
            return lax.dot_general(ref[...], rows_ref[cols, :], nt, preferred_element_type=jnp.float32) * scale

        @pl.when(v < j)
        def _():
            stage_ref[j] = product(own).astype(jnp.bfloat16)

        @pl.when(v > j)
        def _():
            stage_ref[j] = product(im_ref).astype(jnp.bfloat16)

        @pl.when(v == j)
        def _():
            row = lax.broadcasted_iota(jnp.int32, (ROWS, ROWS), 0)
            col = lax.broadcasted_iota(jnp.int32, (ROWS, ROWS), 1)
            stage_ref[j] = jnp.where(col >= row, product(own), product(im_ref)).astype(jnp.bfloat16)

        pltpu.make_async_copy(stage_ref.at[j], out_ref.at[0, :, pl.ds(j * ROWS, ROWS)], sem.at[j]).start()
    for j in range(NV):
        pltpu.make_async_copy(stage_ref.at[j], out_ref.at[0, :, pl.ds(j * ROWS, ROWS)], sem.at[j]).wait()


def correlate(rows):
    return pl.pallas_call(
        correlate_kernel,
        out_shape=jax.ShapeDtypeStruct((1, ROWS, NV * ROWS), jnp.bfloat16),
        in_specs=[pl.BlockSpec(memory_space=pl.ANY)],
        out_specs=pl.BlockSpec(memory_space=pl.ANY),
        scratch_shapes=[
            pltpu.VMEM((ROWS, 256), jnp.bfloat16),
            pltpu.VMEM((NV * ROWS, 256), jnp.bfloat16),
            pltpu.VMEM((ROWS, 256), jnp.bfloat16),
            pltpu.VMEM((NV, ROWS, ROWS), jnp.bfloat16),
            pltpu.SemaphoreType.DMA((NV,)),
            pltpu.SemaphoreType.DMA((NV + 1,)),
        ],
    )(rows)


def channelize_kernel(
    samples_ref, history_ref, taps_ref, kept_ref, out_ref,
    frames_ref, previous_ref, table_ref, weighted_ref, order_ref, wide_ref, z_ref, g_ref, stage_ref, spill_ref, tail_ref, head_ref,
    load_sem, h_send, h_recv, gossip, a_send, a_recv, x_send, x_recv, out_sem,
):
    me = lax.axis_index("inp")
    v = lax.axis_index("vis")
    y, z, c = me // 16, lax.rem(me // 2, 8), lax.rem(me, 2)
    right, left, opp = lax.rem(v + 1, NV), lax.rem(v + 3, NV), lax.rem(v + 2, NV)

    def place(dy, dz, dc):
        return lax.rem(y + dy, 8) * 16 + lax.rem(z + dz, 8) * 2 + lax.rem(c + dc, 2)

    barrier = pltpu.get_barrier_semaphore()

    def greet(dy, _):
        for dc in (0, 1):
            pl.semaphore_signal(barrier, inc=1, device_id=(place(dy, 0, dc), v), device_id_type=MESH)
        return 0

    lax.fori_loop(1, NY, greet, 0)
    for step in ((0, 0, 1), (0, 1, 0), (0, 7, 0)):
        pl.semaphore_signal(barrier, inc=1, device_id=(place(*step), v), device_id_type=MESH)
    for other in (left, right, opp):
        pl.semaphore_signal(barrier, inc=1, device_id=(me, other), device_id_type=MESH)

    load = pltpu.make_async_copy(samples_ref, frames_ref, load_sem.at[0])
    load.start()
    old = pltpu.make_async_copy(history_ref, previous_ref, load_sem.at[1])
    old.start()
    write_order(order_ref)
    write_table(kept_ref, table_ref)
    def tell_z():
        pl.semaphore_signal(gossip.at[0], inc=1, device_id=(place(0, 1, 0), v), device_id_type=MESH)
        pl.semaphore_signal(gossip.at[1], inc=1, device_id=(place(0, 7, 0), v), device_id_type=MESH)

    def hear_z():
        pl.semaphore_wait(gossip.at[0], 1)
        pl.semaphore_wait(gossip.at[1], 1)

    load.wait()
    write_tail(lambda k, cols: frames_ref[FRAMES - TAPS + 1 + k, :, cols], taps_ref, table_ref, spill_ref, tail_ref)
    old.wait()

    @pl.when(v == 0)
    def _():
        write_tail(lambda k, cols: previous_ref[k, :, cols], taps_ref, table_ref, spill_ref, head_ref)

    handover = pltpu.make_async_remote_copy(
        src_ref=tail_ref, dst_ref=head_ref, send_sem=h_send, recv_sem=h_recv, device_id=(me, right), device_id_type=MESH
    )

    filter_frames(frames_ref, taps_ref, weighted_ref, 0, 4)
    pl.semaphore_wait(barrier, 2 * (NY - 1) + 6)
    tell_z()

    @pl.when(v < NV - 1)
    def _():
        handover.start()

    filter_frames(frames_ref, taps_ref, weighted_ref, 4, 16)

    @pl.when(v > 0)
    def _():
        handover.wait_recv()

    write_blocks(table_ref, weighted_ref, head_ref, order_ref, wide_ref, z_ref)

    @pl.when(v < NV - 1)
    def _():
        handover.wait_send()
    own = pltpu.make_async_copy(z_ref.at[me], g_ref.at[v, y, z, c], load_sem.at[2])
    own.start()

    def send(target, dz):
        pltpu.make_async_remote_copy(
            src_ref=z_ref.at[target],
            dst_ref=g_ref.at[v, y, z, c],
            send_sem=a_send,
            recv_sem=a_recv.at[(8 - dz) % 8],
            device_id=(target, v),
            device_id_type=MESH,
        ).start()

    for k, group in enumerate(ZGROUPS):
        bases = [(dz, lax.rem(z + dz, NZ) * 2) for dz in group]
        if k == 0:
            send(place(0, 0, 1), 0)
        else:
            hear_z()
            if k < 4:
                tell_z()

        def body(i, _, bases=bases):
            row = lax.rem(y + 8 + (i + 1) // 2 * (2 * lax.rem(i, 2) - 1), NY) * 16
            for core in (0, 1):
                for dz, base in bases:
                    send(row + base + core, dz)
            return 0

        lax.fori_loop(1 if k == 0 else 0, NY, body, 0)
    own.wait()

    def whole(vv, tz):
        return g_ref.at[vv, :, tz]

    def half(vv, tz, h):
        return g_ref.at[vv, pl.ds(4 * h, 4), tz]

    def relay(k):
        for dz in ZGROUPS[k]:
            if dz in DIRECT:
                continue
            tz = lax.rem(z + dz, 8)
            for side, (source, target) in enumerate(((left, right), (right, left))):
                pltpu.make_async_copy(whole(source, tz), whole(source, tz), x_recv.at[dz, side]).wait()
                pltpu.make_async_remote_copy(
                    src_ref=half(source, tz, side),
                    dst_ref=half(source, tz, side),
                    send_sem=x_send.at[2],
                    recv_sem=x_recv.at[dz, 2 + side],
                    device_id=(me, target),
                    device_id_type=MESH,
                ).start()

    for k, group in enumerate(ZGROUPS):
        for dz in group:
            tz = lax.rem(z + dz, 8)
            if dz == 0:
                pltpu.make_async_copy(z_ref.at[pl.ds(0, 15)], z_ref.at[pl.ds(0, 15)], a_recv.at[0]).wait()
            else:
                pltpu.make_async_copy(whole(v, tz), whole(v, tz), a_recv.at[dz]).wait()
            for side, target in enumerate((right, left)):
                pltpu.make_async_remote_copy(
                    src_ref=whole(v, tz),
                    dst_ref=whole(v, tz),
                    send_sem=x_send.at[side],
                    recv_sem=x_recv.at[dz, side],
                    device_id=(me, target),
                    device_id_type=MESH,
                ).start()
            if dz in DIRECT:
                pltpu.make_async_remote_copy(
                    src_ref=whole(v, tz),
                    dst_ref=whole(v, tz),
                    send_sem=x_send.at[2],
                    recv_sem=x_recv.at[dz, 2],
                    device_id=(me, opp),
                    device_id_type=MESH,
                ).start()
        if k >= DEPTH:
            relay(k - DEPTH)
    for k in range(len(ZGROUPS) - DEPTH, len(ZGROUPS)):
        relay(k)
    low = lax.broadcasted_iota(jnp.int32, (2, 8, 128), 2) < 64
    for k, dz in enumerate(dz for group in ZGROUPS for dz in group):
        tz = lax.rem(z + dz, 8)
        if dz in DIRECT:
            for side, source in enumerate((left, right, opp)):
                pltpu.make_async_copy(whole(source, tz), whole(source, tz), x_recv.at[dz, side]).wait()
        else:
            for side in range(2):
                pltpu.make_async_copy(half(opp, tz, side), half(opp, tz, side), x_recv.at[dz, 2 + side]).wait()

        def rows(row, _, k=k, tz=tz):
            for pair in range(2):
                p = g_ref[2 * pair, row, tz].astype(jnp.float32)
                q = g_ref[2 * pair + 1, row, tz].astype(jnp.float32)
                top = jnp.where(low, p, pltpu.roll(q, 64, 2))
                bottom = jnp.where(low, pltpu.roll(p, 64, 2), q)
                both = jnp.concatenate([top, bottom], axis=1).reshape(32, 128)
                stage_ref[k, row, :, pair * 128 : pair * 128 + 128] = both.astype(jnp.bfloat16)
            return 0

        lax.fori_loop(0, NY, rows, 0)
        pltpu.make_async_copy(stage_ref.at[k], out_ref.at[:, tz], out_sem).start()
    pltpu.make_async_copy(stage_ref, out_ref, out_sem).wait()
    for i in range(3):
        pltpu.make_async_copy(g_ref.at[v], g_ref.at[v], x_send.at[i]).wait()
    pltpu.make_async_copy(z_ref.at[pl.ds(0, NI - 1)], z_ref.at[pl.ds(0, NI - 1)], a_send).wait()


def channelize(samples, history, fir_taps, kept_channels):
    vmem = pl.BlockSpec(memory_space=pltpu.VMEM)
    hbm = pl.BlockSpec(memory_space=pl.ANY)
    return pl.pallas_call(
        channelize_kernel,
        out_shape=jax.ShapeDtypeStruct((NY, NZ, 32, 256), jnp.bfloat16),
        in_specs=[hbm, hbm, vmem, vmem],
        out_specs=hbm,
        scratch_shapes=[
            pltpu.VMEM((FRAMES, 16, SAMPLES), jnp.bfloat16),
            pltpu.VMEM((TAPS - 1, 16, SAMPLES), jnp.bfloat16),
            pltpu.VMEM((2 * NI, SAMPLES), jnp.bfloat16),
            pltpu.VMEM((512, SAMPLES), jnp.bfloat16),
            pltpu.VMEM((512, 512), jnp.bfloat16),
            pltpu.VMEM((1024, 128), jnp.float32),
            pltpu.VMEM((NI, 8, 128), jnp.bfloat16),
            pltpu.VMEM((NV, NY, NZ, 2, 8, 128), jnp.bfloat16),
            pltpu.VMEM((NZ, NY, 32, 256), jnp.bfloat16),
            pltpu.VMEM((48, SAMPLES), jnp.bfloat16),
            pltpu.VMEM((48, 2 * NI), jnp.bfloat16),
            pltpu.VMEM((48, 2 * NI), jnp.bfloat16),
            pltpu.SemaphoreType.DMA((3,)),
            pltpu.SemaphoreType.DMA,
            pltpu.SemaphoreType.DMA,
            pltpu.SemaphoreType.REGULAR((2,)),
            pltpu.SemaphoreType.DMA,
            pltpu.SemaphoreType.DMA((8,)),
            pltpu.SemaphoreType.DMA((3,)),
            pltpu.SemaphoreType.DMA((8, 4)),
            pltpu.SemaphoreType.DMA,
        ],
        compiler_params=pltpu.CompilerParams(collective_id=0, has_side_effects=True),
    )(samples, history, fir_taps, kept_channels.reshape(1, NI))


def per_device(samples, history, fir_taps, kept_channels):
    rows = channelize(samples, history, fir_taps, kept_channels)
    return correlate(rows.reshape(NV * ROWS, 256))


def solution(mesh):
    return jax.shard_map(
        per_device,
        mesh=mesh,
        in_specs=(P("vis", "inp", None), P(None, "inp", None), P(), P()),
        out_specs=P("inp", "vis", None),
        check_vma=False,
    )
```

```python
import functools
import math

import jax
import jax.numpy as jnp
from jax import lax
from jax.experimental import pallas as pl
from jax.experimental.pallas import tpu as pltpu
from jax.sharding import PartitionSpec as P

TAPS = 4
SAMPLES, FRAMES, ROWS = 2048, 32, 512
MESH = pl.DeviceIdType.MESH
NI, NV, NY, NZ = 128, 4, 8, 8
ZGROUPS = ((0,), (1, 7), (2, 6), (3, 5), (4,))
DEPTH = 1
DIRECT = (0, 1, 2, 3, 4, 5, 6, 7)


def trig(m):
    quadrant = (m + 256) >> 9
    x = (m - (quadrant << 9)).astype(jnp.float32) * (2.0 * math.pi / SAMPLES)
    s = x * x
    c = 1.0 + s * (-0.5 + s * (1.0 / 24 + s * (-1.0 / 720 + s * (1.0 / 40320))))
    d = x * (1.0 + s * (-1.0 / 6 + s * (1.0 / 120 + s * (-1.0 / 5040 + s * (1.0 / 362880)))))
    odd = (quadrant & 1) == 1
    cos = jnp.where(odd, d, c)
    sin = jnp.where(odd, c, d)
    cos = jnp.where((quadrant == 1) | (quadrant == 2), -cos, cos)
    sin = jnp.where((quadrant == 2) | (quadrant == 3), -sin, sin)
    return cos, sin


def write_table(kept_ref, table_ref):
    lane = lax.broadcasted_iota(jnp.int32, (NI, 128), 1)
    here = lane == lax.broadcasted_iota(jnp.int32, (NI, 128), 0)
    kept = jnp.broadcast_to(kept_ref[...], (NI, 128)).astype(jnp.float32)
    kept = jnp.sum(jnp.where(here, kept, 0.0), axis=1, keepdims=True).astype(jnp.int32)
    cl, sl = trig((kept * lane) & (SAMPLES - 1))
    ch, sh = trig((kept * lane * 128) & (SAMPLES - 1))
    scale = 1.0 / math.sqrt(SAMPLES)
    cl, sl = cl * scale, sl * scale
    for high in range(SAMPLES // 128):
        a = jnp.broadcast_to(ch[:, high : high + 1], (NI, 128))
        b = jnp.broadcast_to(sh[:, high : high + 1], (NI, 128))
        cols = slice(high * 128, high * 128 + 128)
        table_ref[0:NI, cols] = (a * cl - b * sl).astype(jnp.bfloat16)
        table_ref[NI:, cols] = (-(b * cl) - a * sl).astype(jnp.bfloat16)


def write_order(order_ref):
    m = lax.broadcasted_iota(jnp.int32, (512, 512), 0)
    t = lax.broadcasted_iota(jnp.int32, (512, 512), 1)
    source = ((t & 31) << 4) | (((t >> 6) & 1) << 3) | ((t >> 7) << 1) | ((t >> 5) & 1)
    order_ref[...] = jnp.where(m == source, 1.0, 0.0).astype(jnp.bfloat16)


def filter_frames(source_ref, taps_ref, weighted_ref, lo, hi):
    def chunk(j, _):
        cols = pl.ds(pl.multiple_of(j * 128, 128), 128)
        taps = [jnp.broadcast_to(taps_ref[t : t + 1, cols], (16, 128)) for t in range(TAPS)]
        window = []
        for f in range(FRAMES):
            window.append(source_ref[f, :, cols].astype(jnp.float32))
            window = window[-TAPS:]
            terms = taps[TAPS - len(window) :]
            total = terms[0] * window[0]
            for t in range(1, len(window)):
                total = total + terms[t] * window[t]
            weighted_ref[f * 16 : f * 16 + 16, cols] = total.astype(jnp.bfloat16)
        return 0

    lax.fori_loop(lo, hi, chunk, 0)


def write_tail(last, taps_ref, table_ref, spill_ref, tail_ref):
    def chunk(j, _):
        cols = pl.ds(pl.multiple_of(j * 128, 128), 128)
        taps = [jnp.broadcast_to(taps_ref[t : t + 1, cols], (16, 128)) for t in range(TAPS - 1)]
        window = [last(k, cols).astype(jnp.float32) for k in range(TAPS - 1)]
        for f in range(TAPS - 1):
            total = taps[0] * window[f]
            for t in range(1, TAPS - 1 - f):
                total = total + taps[t] * window[f + t]
            spill_ref[f * 16 : f * 16 + 16, cols] = total.astype(jnp.bfloat16)
        return 0

    lax.fori_loop(0, SAMPLES // 128, chunk, 0)
    nt = (((1,), (1,)), ((), ()))
    tail = lax.dot_general(spill_ref[...], table_ref[...], nt, preferred_element_type=jnp.float32)
    tail_ref[...] = tail.astype(jnp.bfloat16)


def write_blocks(table_ref, weighted_ref, head_ref, order_ref, wide_ref, z_ref):
    nt = (((1,), (1,)), ((), ()))
    spectra = lax.dot_general(table_ref[...], weighted_ref[...], nt, preferred_element_type=jnp.float32)
    count = (TAPS - 1) * 16
    place = lax.broadcasted_iota(jnp.int32, (count, 128), 0) == lax.broadcasted_iota(jnp.int32, (count, 128), 1)
    place = jnp.where(place, 1.0, 0.0).astype(jnp.bfloat16)
    tn = (((0,), (0,)), ((), ()))
    first = spectra[:, 0:128] + lax.dot_general(head_ref[...], place, tn, preferred_element_type=jnp.float32)
    spectra = jnp.concatenate([first, spectra[:, 128:]], axis=1).astype(jnp.bfloat16)
    spectra = jnp.dot(spectra, order_ref[...], preferred_element_type=jnp.float32)
    even = (lax.broadcasted_iota(jnp.int32, (NI, 128), 1) & 32) == 0
    for pair in range(4):
        cols = slice(pair * 128, pair * 128 + 128)
        re, im = spectra[0:NI, cols], spectra[NI:, cols]
        wide_ref[pl.ds(2 * pair, NI, stride=8), :] = jnp.where(even, re, pltpu.roll(im, 32, 1))
        wide_ref[pl.ds(2 * pair + 1, NI, stride=8), :] = jnp.where(even, pltpu.roll(re, 96, 1), im)
    z_ref[...] = wide_ref[...].reshape(NI, 8, 128).astype(jnp.bfloat16)


def correlate_kernel(source_ref, out_ref, own, rows_ref, im_ref, stage_ref, sem, load_sem):
    v = lax.axis_index("vis")
    mine = pltpu.make_async_copy(source_ref.at[pl.ds(pl.multiple_of(v * ROWS, ROWS), ROWS)], own, load_sem.at[NV])
    mine.start()
    loads = []
    for j in range(NV):
        block = pl.ds(j * ROWS, ROWS)
        loads.append(pltpu.make_async_copy(source_ref.at[block], rows_ref.at[block], load_sem.at[j]))
        loads[j].start()
    mine.wait()
    real = (lax.broadcasted_iota(jnp.int32, (ROWS, 128), 1) & 32) == 0
    for pair in range(2):
        x = own[:, pair * 128 : pair * 128 + 128].astype(jnp.float32)
        turned = jnp.where(real, pltpu.roll(x, 96, 1), -pltpu.roll(x, 32, 1))
        im_ref[:, pair * 128 : pair * 128 + 128] = turned.astype(jnp.bfloat16)

    nt = (((1,), (1,)), ((), ()))
    scale = 1.0 / (NV * FRAMES)
    for j in range(NV):
        cols = slice(j * ROWS, j * ROWS + ROWS)
        loads[j].wait()

        def product(ref, cols=cols):
            return lax.dot_general(ref[...], rows_ref[cols, :], nt, preferred_element_type=jnp.float32) * scale

        @pl.when(v < j)
        def _():
            stage_ref[j] = product(own).astype(jnp.bfloat16)

        @pl.when(v > j)
        def _():
            stage_ref[j] = product(im_ref).astype(jnp.bfloat16)

        @pl.when(v == j)
        def _():
            row = lax.broadcasted_iota(jnp.int32, (ROWS, ROWS), 0)
            col = lax.broadcasted_iota(jnp.int32, (ROWS, ROWS), 1)
            stage_ref[j] = jnp.where(col >= row, product(own), product(im_ref)).astype(jnp.bfloat16)

        pltpu.make_async_copy(stage_ref.at[j], out_ref.at[0, :, pl.ds(j * ROWS, ROWS)], sem.at[j]).start()
    for j in range(NV):
        pltpu.make_async_copy(stage_ref.at[j], out_ref.at[0, :, pl.ds(j * ROWS, ROWS)], sem.at[j]).wait()


def correlate(rows):
    return pl.pallas_call(
        correlate_kernel,
        out_shape=jax.ShapeDtypeStruct((1, ROWS, NV * ROWS), jnp.bfloat16),
        in_specs=[pl.BlockSpec(memory_space=pl.ANY)],
        out_specs=pl.BlockSpec(memory_space=pl.ANY),
        scratch_shapes=[
            pltpu.VMEM((ROWS, 256), jnp.bfloat16),
            pltpu.VMEM((NV * ROWS, 256), jnp.bfloat16),
            pltpu.VMEM((ROWS, 256), jnp.bfloat16),
            pltpu.VMEM((NV, ROWS, ROWS), jnp.bfloat16),
            pltpu.SemaphoreType.DMA((NV,)),
            pltpu.SemaphoreType.DMA((NV + 1,)),
        ],
    )(rows)


def channelize_kernel(
    samples_ref, history_ref, taps_ref, kept_ref, out_ref,
    frames_ref, previous_ref, table_ref, weighted_ref, order_ref, wide_ref, z_ref, g_ref, stage_ref, spill_ref, tail_ref, head_ref,
    load_sem, h_send, h_recv, gossip, a_send, a_recv, x_send, x_recv, out_sem,
):
    me = lax.axis_index("inp")
    v = lax.axis_index("vis")
    y, z, c = me // 16, lax.rem(me // 2, 8), lax.rem(me, 2)
    right, left, opp = lax.rem(v + 1, NV), lax.rem(v + 3, NV), lax.rem(v + 2, NV)

    def place(dy, dz, dc):
        return lax.rem(y + dy, 8) * 16 + lax.rem(z + dz, 8) * 2 + lax.rem(c + dc, 2)

    barrier = pltpu.get_barrier_semaphore()

    def greet(dy, _):
        for dc in (0, 1):
            pl.semaphore_signal(barrier, inc=1, device_id=(place(dy, 0, dc), v), device_id_type=MESH)
        return 0

    lax.fori_loop(1, NY, greet, 0)
    for step in ((0, 0, 1), (0, 1, 0), (0, 7, 0)):
        pl.semaphore_signal(barrier, inc=1, device_id=(place(*step), v), device_id_type=MESH)
    for other in (left, right, opp):
        pl.semaphore_signal(barrier, inc=1, device_id=(me, other), device_id_type=MESH)

    load = pltpu.make_async_copy(samples_ref, frames_ref, load_sem.at[0])
    load.start()
    old = pltpu.make_async_copy(history_ref, previous_ref, load_sem.at[1])
    old.start()
    write_order(order_ref)
    write_table(kept_ref, table_ref)
    def tell_z():
        pl.semaphore_signal(gossip.at[0], inc=1, device_id=(place(0, 1, 0), v), device_id_type=MESH)
        pl.semaphore_signal(gossip.at[1], inc=1, device_id=(place(0, 7, 0), v), device_id_type=MESH)

    def hear_z():
        pl.semaphore_wait(gossip.at[0], 1)
        pl.semaphore_wait(gossip.at[1], 1)

    load.wait()
    write_tail(lambda k, cols: frames_ref[FRAMES - TAPS + 1 + k, :, cols], taps_ref, table_ref, spill_ref, tail_ref)
    old.wait()

    @pl.when(v == 0)
    def _():
        write_tail(lambda k, cols: previous_ref[k, :, cols], taps_ref, table_ref, spill_ref, head_ref)

    handover = pltpu.make_async_remote_copy(
        src_ref=tail_ref, dst_ref=head_ref, send_sem=h_send, recv_sem=h_recv, device_id=(me, right), device_id_type=MESH
    )

    pl.semaphore_wait(barrier, 2 * (NY - 1) + 6)
    tell_z()

    @pl.when(v < NV - 1)
    def _():
        handover.start()

    filter_frames(frames_ref, taps_ref, weighted_ref, 0, 16)

    @pl.when(v > 0)
    def _():
        handover.wait_recv()

    write_blocks(table_ref, weighted_ref, head_ref, order_ref, wide_ref, z_ref)

    @pl.when(v < NV - 1)
    def _():
        handover.wait_send()
    own = pltpu.make_async_copy(z_ref.at[me], g_ref.at[v, y, z, c], load_sem.at[2])
    own.start()

    def send(target, dz):
        pltpu.make_async_remote_copy(
            src_ref=z_ref.at[target],
            dst_ref=g_ref.at[v, y, z, c],
            send_sem=a_send,
            recv_sem=a_recv.at[(8 - dz) % 8],
            device_id=(target, v),
            device_id_type=MESH,
        ).start()

    for k, group in enumerate(ZGROUPS):
        bases = [(dz, lax.rem(z + dz, NZ) * 2) for dz in group]
        if k == 0:
            send(place(0, 0, 1), 0)
        else:
            hear_z()
            if k < 4:
                tell_z()

        def body(i, _, bases=bases):
            row = lax.rem(y + 8 + (i + 1) // 2 * (2 * lax.rem(i, 2) - 1), NY) * 16
            for core in (0, 1):
                for dz, base in bases:
                    send(row + base + core, dz)
            return 0

        lax.fori_loop(1 if k == 0 else 0, NY, body, 0)
    own.wait()

    def whole(vv, tz):
        return g_ref.at[vv, :, tz]

    def half(vv, tz, h):
        return g_ref.at[vv, pl.ds(4 * h, 4), tz]

    def relay(k):
        for dz in ZGROUPS[k]:
            if dz in DIRECT:
                continue
            tz = lax.rem(z + dz, 8)
            for side, (source, target) in enumerate(((left, right), (right, left))):
                pltpu.make_async_copy(whole(source, tz), whole(source, tz), x_recv.at[dz, side]).wait()
                pltpu.make_async_remote_copy(
                    src_ref=half(source, tz, side),
                    dst_ref=half(source, tz, side),
                    send_sem=x_send.at[2],
                    recv_sem=x_recv.at[dz, 2 + side],
                    device_id=(me, target),
                    device_id_type=MESH,
                ).start()

    for k, group in enumerate(ZGROUPS):
        for dz in group:
            tz = lax.rem(z + dz, 8)
            if dz == 0:
                pltpu.make_async_copy(z_ref.at[pl.ds(0, 15)], z_ref.at[pl.ds(0, 15)], a_recv.at[0]).wait()
            else:
                pltpu.make_async_copy(whole(v, tz), whole(v, tz), a_recv.at[dz]).wait()
            for side, target in enumerate((right, left)):
                pltpu.make_async_remote_copy(
                    src_ref=whole(v, tz),
                    dst_ref=whole(v, tz),
                    send_sem=x_send.at[side],
                    recv_sem=x_recv.at[dz, side],
                    device_id=(me, target),
                    device_id_type=MESH,
                ).start()
            if dz in DIRECT:
                pltpu.make_async_remote_copy(
                    src_ref=whole(v, tz),
                    dst_ref=whole(v, tz),
                    send_sem=x_send.at[2],
                    recv_sem=x_recv.at[dz, 2],
                    device_id=(me, opp),
                    device_id_type=MESH,
                ).start()
        if k >= DEPTH:
            relay(k - DEPTH)
    for k in range(len(ZGROUPS) - DEPTH, len(ZGROUPS)):
        relay(k)
    low = lax.broadcasted_iota(jnp.int32, (2, 8, 128), 2) < 64
    for k, dz in enumerate(dz for group in ZGROUPS for dz in group):
        tz = lax.rem(z + dz, 8)
        if dz in DIRECT:
            for side, source in enumerate((left, right, opp)):
                pltpu.make_async_copy(whole(source, tz), whole(source, tz), x_recv.at[dz, side]).wait()
        else:
            for side in range(2):
                pltpu.make_async_copy(half(opp, tz, side), half(opp, tz, side), x_recv.at[dz, 2 + side]).wait()

        def rows(row, _, k=k, tz=tz):
            for pair in range(2):
                p = g_ref[2 * pair, row, tz].astype(jnp.float32)
                q = g_ref[2 * pair + 1, row, tz].astype(jnp.float32)
                top = jnp.where(low, p, pltpu.roll(q, 64, 2))
                bottom = jnp.where(low, pltpu.roll(p, 64, 2), q)
                both = jnp.concatenate([top, bottom], axis=1).reshape(32, 128)
                stage_ref[k, row, :, pair * 128 : pair * 128 + 128] = both.astype(jnp.bfloat16)
            return 0

        lax.fori_loop(0, NY, rows, 0)
        pltpu.make_async_copy(stage_ref.at[k], out_ref.at[:, tz], out_sem).start()
    pltpu.make_async_copy(stage_ref, out_ref, out_sem).wait()
    for i in range(3):
        pltpu.make_async_copy(g_ref.at[v], g_ref.at[v], x_send.at[i]).wait()
    pltpu.make_async_copy(z_ref.at[pl.ds(0, NI - 1)], z_ref.at[pl.ds(0, NI - 1)], a_send).wait()


def channelize(samples, history, fir_taps, kept_channels):
    vmem = pl.BlockSpec(memory_space=pltpu.VMEM)
    hbm = pl.BlockSpec(memory_space=pl.ANY)
    return pl.pallas_call(
        channelize_kernel,
        out_shape=jax.ShapeDtypeStruct((NY, NZ, 32, 256), jnp.bfloat16),
        in_specs=[hbm, hbm, vmem, vmem],
        out_specs=hbm,
        scratch_shapes=[
            pltpu.VMEM((FRAMES, 16, SAMPLES), jnp.bfloat16),
            pltpu.VMEM((TAPS - 1, 16, SAMPLES), jnp.bfloat16),
            pltpu.VMEM((2 * NI, SAMPLES), jnp.bfloat16),
            pltpu.VMEM((512, SAMPLES), jnp.bfloat16),
            pltpu.VMEM((512, 512), jnp.bfloat16),
            pltpu.VMEM((1024, 128), jnp.float32),
            pltpu.VMEM((NI, 8, 128), jnp.bfloat16),
            pltpu.VMEM((NV, NY, NZ, 2, 8, 128), jnp.bfloat16),
            pltpu.VMEM((NZ, NY, 32, 256), jnp.bfloat16),
            pltpu.VMEM((48, SAMPLES), jnp.bfloat16),
            pltpu.VMEM((48, 2 * NI), jnp.bfloat16),
            pltpu.VMEM((48, 2 * NI), jnp.bfloat16),
            pltpu.SemaphoreType.DMA((3,)),
            pltpu.SemaphoreType.DMA,
            pltpu.SemaphoreType.DMA,
            pltpu.SemaphoreType.REGULAR((2,)),
            pltpu.SemaphoreType.DMA,
            pltpu.SemaphoreType.DMA((8,)),
            pltpu.SemaphoreType.DMA((3,)),
            pltpu.SemaphoreType.DMA((8, 4)),
            pltpu.SemaphoreType.DMA,
        ],
        compiler_params=pltpu.CompilerParams(collective_id=0, has_side_effects=True),
    )(samples, history, fir_taps, kept_channels.reshape(1, NI))


def per_device(samples, history, fir_taps, kept_channels):
    rows = channelize(samples, history, fir_taps, kept_channels)
    return correlate(rows.reshape(NV * ROWS, 256))


def solution(mesh):
    return jax.shard_map(
        per_device,
        mesh=mesh,
        in_specs=(P("vis", "inp", None), P(None, "inp", None), P(), P()),
        out_specs=P("inp", "vis", None),
        check_vma=False,
    )
```
